512 devices in a mesh: rows: 64 (over z, y_hi, core), chan: 8 (over y_lo, x).
Axes of the slice: x: 4, y: 8 (y_hi: 4, y_lo: 2; y = y_hi * 2 + y_lo), z: 8, core: 2. Of those that a mesh axis runs over, the one named last changes fastest.
Arguments:
- pair: bfloat16 [512, 512, 128], P('rows', 'chan'), may hold values from -6 to 6
- block_mask: int32 [4, 4], replicated, may hold values from 0 to 1, as said below
- w_in: bfloat16 [128, 640], replicated, may hold values from -0.5 to 0.5
- w_out: bfloat16 [128, 128], replicated, may hold values from -0.5 to 0.5
Outputs:
- update: bfloat16 [512, 512, 128], P('rows', 'chan')
The draws below stay inside these ranges and needn't reach their ends.
Inputs may be any that keep to these rules, and one draw needn't show every extreme that they name: Every diagonal entry of block_mask is 1; other entries are 0 or 1.
All inputs are finite; a program needn't handle non-finite values.
Results may differ from the reference program's by a relative error of at most 0.0078.
Values may be sent and summed in bfloat16 or wider, within the bound.
A program may use at most 64 MiB of HBM per device.

```python
import jax
import jax.numpy as jnp
from jax import lax

C = 128
BLOCK = 128
TOKENS = 512


def draw_block_mask(key, part):
    blocks = TOKENS // BLOCK
    values = jax.random.randint(key, (blocks, blocks), 0, 10)
    first = lax.broadcasted_iota(jnp.int32, (blocks, blocks), 0)
    second = lax.broadcasted_iota(jnp.int32, (blocks, blocks), 1)
    return jnp.where((first == second) | (values < 3), 1, 0).astype(jnp.int32)


def level_of(rng, extent, split, smallest, largest):
    factor_of, own = 1.0, jax.random.fold_in(rng, 6)
    for axis_at, shards_of in split:
        steps = jnp.exp(jax.random.uniform(jax.random.fold_in(own, axis_at), (shards_of,), jnp.float32, smallest / len(split), largest / len(split)))
        factor_of = factor_of * jnp.repeat(steps, extent[axis_at] // shards_of).reshape([-1 if axis == axis_at else 1 for axis in range(len(extent))])
    return factor_of


def noise(stream_key, extent, spread, reach, shards=(), dtype=jnp.bfloat16):
    values = spread * jax.random.normal(stream_key, extent, jnp.float32)
    if shards:
        values = values * level_of(stream_key, extent, shards, -0.22, 0.18)
    return jnp.clip(values, -reach, reach).astype(dtype)


def setup_inputs(seed: int = 0) -> dict:
    splits = jax.random.split(jax.random.key(seed), 5)
    pair = noise(splits[0], (TOKENS, TOKENS, C), 1.0, 6.0, ((0, 64), (1, 8)))
    block_mask = draw_block_mask(jax.random.fold_in(splits[4], 71), 0)
    w_in = noise(splits[2], (C, 5 * C), C ** -0.5, 0.5)
    w_out = noise(splits[3], (C, C), C ** -0.5, 0.5)
    return {"pair": pair, "block_mask": block_mask, "w_in": w_in, "w_out": w_out}


def layer_norm(values):
    mean = lax.optimization_barrier(jnp.mean(values, axis=-1, keepdims=True))
    centered = values - mean
    var = lax.optimization_barrier(jnp.mean(centered * centered, axis=-1, keepdims=True))
    return centered / jnp.sqrt(var + 1e-05)

def reference(pair, block_mask, w_in, w_out):
    count = pair.shape[0]
    width = pair.shape[2]
    normed = layer_norm(pair.astype(jnp.float32)).astype(jnp.bfloat16)
    proj = jnp.dot(normed.reshape(-1, width), w_in, preferred_element_type=jnp.float32).reshape(count, count, 5 * width)
    mask = jnp.repeat(jnp.repeat(block_mask.astype(jnp.float32), BLOCK, axis=0), BLOCK, axis=1)[:, :, None]
    left = (jax.nn.sigmoid(proj[..., :width]) * proj[..., width:2 * width] * mask).astype(jnp.bfloat16)
    right = (jax.nn.sigmoid(proj[..., 2 * width:3 * width]) * proj[..., 3 * width:4 * width] * mask).astype(jnp.bfloat16)
    gate = jax.nn.sigmoid(proj[..., 4 * width:])
    left_t = jnp.transpose(left, (2, 0, 1)).astype(jnp.float32)
    right_t = jnp.transpose(right, (2, 0, 1)).astype(jnp.float32)
    prod = jnp.einsum('cik,cjk->cij', left_t, right_t)
    prod = jnp.transpose(prod, (1, 2, 0))
    normed_prod = layer_norm(prod).astype(jnp.bfloat16)
    mixed = jnp.dot(normed_prod.reshape(-1, width), w_out, preferred_element_type=jnp.float32).reshape(count, count, width)
    return (gate * mixed).astype(jnp.bfloat16)
```

```python
import functools

import jax
import jax.numpy as jnp
from jax import lax
from jax.experimental import pallas as pl
from jax.experimental.pallas import tpu as pltpu
from jax.sharding import PartitionSpec as P

BLOCK = 128
EPS = 1e-05
MESH = pl.DeviceIdType.MESH
NT = (((1,), (1,)), ((), ()))


def wait_bytes(ref, sem):
    pltpu.make_async_copy(ref, ref, sem).wait()


def kernel(
    n_z, n_rs, n_q,
    mask_ref, pair_ref, w_in_ref, w_out_ref, out_ref,
    stage, send_l, send_r, l_in, r_all, l_mat, out_send, prod_in, gate,
    a2a_send, a2a_recv, ring_send, ring_recv, out_sems,
):
    n_i, n_k, width = pair_ref.shape
    half = width // 2
    n_plane = n_rs * n_q
    row_at = lax.axis_index("rows")
    q = lax.axis_index("chan")
    z = row_at // n_rs
    rs = row_at % n_rs
    me = rs * n_q + q
    up = {"rows": lax.rem(z + 1, n_z) * n_rs + rs, "chan": q}
    down = {"rows": lax.rem(z + n_z - 1, n_z) * n_rs + rs, "chan": q}

    def plane_device(index):
        return {"rows": z * n_rs + index // n_q, "chan": index % n_q}

    barrier = pltpu.get_barrier_semaphore()

    @pl.loop(1, n_plane)
    def _(step):
        pl.semaphore_signal(
            barrier, inc=1, device_id=plane_device(lax.rem(me + step, n_plane)), device_id_type=MESH
        )

    for neighbour in (up, down):
        pl.semaphore_signal(barrier, inc=1, device_id=neighbour, device_id_type=MESH)

    cells = pair_ref[...].astype(jnp.float32).reshape(n_i * n_k, width)
    mean = jnp.mean(cells, axis=-1, keepdims=True)
    centered = cells - mean
    var = jnp.mean(centered * centered, axis=-1, keepdims=True)
    normed = (centered / jnp.sqrt(var + EPS)).astype(jnp.bfloat16)
    zeros = jnp.zeros((n_k, width), jnp.bfloat16)
    diag = jnp.concatenate(
        [
            jnp.concatenate(pieces, axis=1)
            for i in range(n_i)
            for block in (normed[i * n_k : (i + 1) * n_k],)
            for pieces in ((block, zeros), (zeros, block))
        ],
        axis=0,
    )
    w_t = w_in_ref[:, : 4 * width].astype(jnp.float32).T.astype(jnp.bfloat16)
    w_lhs = jnp.concatenate(
        [
            jnp.concatenate(
                [w_t[p * width : p * width + half], w_t[p * width + half : (p + 1) * width]], axis=1
            )
            for p in range(4)
        ],
        axis=0,
    )
    proj = lax.dot_general(w_lhs, diag, NT, preferred_element_type=jnp.float32)
    cell_mask = mask_ref[(row_at * n_i) // BLOCK, (q * n_k) // BLOCK].astype(jnp.float32)
    for part, ref in ((2, send_r), (0, send_l)):
        gated = (
            jax.nn.sigmoid(proj[part * half : (part + 1) * half])
            * proj[(part + 1) * half : (part + 2) * half]
            * cell_mask
        )
        for i in range(n_i):
            stage[pl.ds(i, half, stride=n_i), :] = gated[:, i * 2 * n_k : (i + 1) * 2 * n_k]
        ref[...] = stage[...].astype(jnp.bfloat16).reshape(ref.shape)

    pl.semaphore_wait(barrier, n_plane + 1)

    def exchange(src, dst, which):
        @pl.loop(1, n_plane)
        def _(step):
            target = lax.rem(me + step, n_plane)
            pltpu.make_async_remote_copy(
                src_ref=src.at[target],
                dst_ref=dst,
                send_sem=a2a_send.at[which],
                recv_sem=a2a_recv.at[which],
                device_id=plane_device(target),
                device_id_type=MESH,
            ).start()

        pltpu.make_async_copy(src.at[me], dst, a2a_recv.at[which]).start()

    exchange(send_r, r_all.at[z, q, rs], 0)
    exchange(send_l, l_in.at[q, rs], 1)

    gate[...] = jax.nn.sigmoid(
        jnp.dot(normed, w_in_ref[:, 4 * width :], preferred_element_type=jnp.float32)
    )

    far = n_z // 2
    n_chunks = 2
    q_chunk = n_q // n_chunks

    def ring_copy(direction, step, chunk):
        block = lax.rem(z + (n_z - step if direction == 0 else step), n_z)
        ref = r_all.at[block, pl.ds(chunk * q_chunk, q_chunk)]
        return pltpu.make_async_remote_copy(
            src_ref=ref,
            dst_ref=ref,
            send_sem=ring_send.at[direction, step, chunk],
            recv_sem=ring_recv.at[direction, step, chunk],
            device_id=up if direction == 0 else down,
            device_id_type=MESH,
        )

    def ring_arrival(direction, step, chunk):
        block = lax.rem(z + (n_z - step if direction == 0 else step), n_z)
        ref = r_all.at[block, pl.ds(chunk * q_chunk, q_chunk)]
        return pltpu.make_async_remote_copy(
            src_ref=ref,
            dst_ref=ref,
            send_sem=ring_send.at[direction, step - 1, chunk],
            recv_sem=ring_recv.at[direction, step - 1, chunk],
            device_id=up if direction == 0 else down,
            device_id_type=MESH,
        )

    def carried(direction, step):
        if step + 1 < far:
            return range(n_chunks)
        return range(0, n_chunks // 2) if direction == 0 else range(n_chunks // 2, n_chunks)

    wait_bytes(r_all.at[z], a2a_recv.at[0])
    started = []
    for chunk in range(n_chunks):
        for direction in (0, 1):
            if chunk in carried(direction, 0):
                ring_copy(direction, 0, chunk).start()
                started.append((direction, 0, chunk))

    wait_bytes(l_in, a2a_recv.at[1])
    low = lax.broadcasted_iota(jnp.int32, (n_rs * n_i, 2 * n_k), 1) < n_k
    for k in range(n_q):
        block = l_in[k].reshape(n_rs * n_i, 2 * n_k).astype(jnp.float32)
        both = jnp.concatenate([jnp.where(low, block, 0.0), jnp.where(low, 0.0, block)], axis=0)
        l_mat[:, k * 2 * n_k : (k + 1) * 2 * n_k] = both.astype(jnp.bfloat16)

    def multiply(block, slot):
        right = jnp.concatenate(
            [r_all[block, k].reshape(n_rs * n_i, 2 * n_k) for k in range(n_q)], axis=1
        )
        prod = lax.dot_general(l_mat[...], right, NT, preferred_element_type=jnp.float32)
        rows = n_rs * n_i
        joined = jnp.concatenate([prod[:rows], prod[rows:]], axis=1).astype(jnp.bfloat16)
        out_send[slot] = joined.reshape(n_rs, n_i, 2 * n_k)

        @pl.loop(0, n_rs)
        def _(step):
            target = lax.rem(rs + step, n_rs)
            local = jnp.logical_and(target == rs, block == q)

            @pl.when(local)
            def _():
                pltpu.make_async_copy(
                    out_send.at[slot, target], prod_in.at[me], out_sems.at[1]
                ).start()

            @pl.when(jnp.logical_not(local))
            def _():
                pltpu.make_async_remote_copy(
                    src_ref=out_send.at[slot, target],
                    dst_ref=prod_in.at[me],
                    send_sem=out_sems.at[0],
                    recv_sem=out_sems.at[1],
                    device_id={"rows": z * n_rs + target, "chan": block},
                    device_id_type=MESH,
                ).start()

    multiply(z, 0)
    for step in range(1, far + 1):
        for chunk in range(n_chunks):
            for direction in (0, 1):
                if chunk in carried(direction, step - 1):
                    ring_arrival(direction, step, chunk).wait_recv()
                    if step < far and chunk in carried(direction, step):
                        ring_copy(direction, step, chunk).start()
                        started.append((direction, step, chunk))
        if step < far:
            multiply(lax.rem(z + n_z - step, n_z), 2 * step - 1)
            multiply(lax.rem(z + step, n_z), 2 * step)
        else:
            multiply(lax.rem(z + step, n_z), 2 * step - 1)

    w_halves = jnp.concatenate([w_out_ref[:half], w_out_ref[half:]], axis=1)
    wait_bytes(prod_in, out_sems.at[1])
    stage[...] = prod_in[...].astype(jnp.float32).reshape(n_plane * n_i, 2 * n_k)
    turned = []
    for i in range(n_i):
        values = stage[pl.ds(i, half, stride=n_i), :]
        total = jnp.sum(values, axis=0, keepdims=True)
        mean = (total + pltpu.roll(total, n_k, 1)) * (1.0 / width)
        centered = values - mean
        square = jnp.sum(centered * centered, axis=0, keepdims=True)
        var = (square + pltpu.roll(square, n_k, 1)) * (1.0 / width)
        turned.append((centered / jnp.sqrt(var + EPS)).T.astype(jnp.bfloat16))
    mixed = jnp.dot(
        jnp.concatenate(turned, axis=0), w_halves, preferred_element_type=jnp.float32
    )
    for i in range(n_i):
        at = i * 2 * n_k
        summed = mixed[at : at + n_k, :width] + mixed[at + n_k : at + 2 * n_k, width:]
        out_ref[i] = (gate[i * n_k : (i + 1) * n_k] * summed).astype(jnp.bfloat16)

    others = pl.ds(0, n_plane - 1)
    wait_bytes(send_r.at[others], a2a_send.at[0])
    wait_bytes(send_l.at[others], a2a_send.at[1])
    for key in started:
        ring_copy(*key).wait_send()

    wait_bytes(prod_in.at[others], out_sems.at[0])


def solution(mesh):
    n_rows, n_q = mesh.shape["rows"], mesh.shape["chan"]

    def on_device(pair, block_mask, w_in, w_out):
        n_i, n_k, width = pair.shape
        half = width // 2
        n_rs = half // n_q
        n_z = n_rows // n_rs
        n_plane = n_rs * n_q
        tile = (n_i, 2 * n_k)
        vmem = pl.BlockSpec(memory_space=pltpu.VMEM)
        return pl.pallas_call(
            functools.partial(kernel, n_z, n_rs, n_q),
            out_shape=jax.ShapeDtypeStruct((n_i, n_k, width), jnp.bfloat16),
            in_specs=[pl.BlockSpec(memory_space=pltpu.SMEM), vmem, vmem, vmem],
            out_specs=vmem,
            scratch_shapes=[
                pltpu.VMEM((n_plane * n_i, 2 * n_k), jnp.float32),
                pltpu.VMEM((n_plane, *tile), jnp.bfloat16),
                pltpu.VMEM((n_plane, *tile), jnp.bfloat16),
                pltpu.VMEM((n_q, n_rs, *tile), jnp.bfloat16),
                pltpu.VMEM((n_z, n_q, n_rs, *tile), jnp.bfloat16),
                pltpu.VMEM((2 * n_rs * n_i, n_q * 2 * n_k), jnp.bfloat16),
                pltpu.VMEM((n_z, n_rs, *tile), jnp.bfloat16),
                pltpu.VMEM((n_plane, *tile), jnp.bfloat16),
                pltpu.VMEM((n_i * n_k, width), jnp.float32),
                pltpu.SemaphoreType.DMA((2,)),
                pltpu.SemaphoreType.DMA((2,)),
                pltpu.SemaphoreType.DMA((2, n_z // 2, 2)),
                pltpu.SemaphoreType.DMA((2, n_z // 2, 2)),
                pltpu.SemaphoreType.DMA((2,)),
            ],
            compiler_params=pltpu.CompilerParams(collective_id=0, has_side_effects=True),
        )(block_mask, pair, w_in, w_out)

    placed = (P("rows", "chan", None), P(), P(), P())
    return jax.shard_map(
        on_device, mesh=mesh, in_specs=placed, out_specs=P("rows", "chan", None), check_vma=False
    )
```

```python
import functools

import jax
import jax.numpy as jnp
from jax import lax
from jax.experimental import pallas as pl
from jax.experimental.pallas import tpu as pltpu
from jax.sharding import PartitionSpec as P

BLOCK = 128
EPS = 1e-05
MESH = pl.DeviceIdType.MESH
NT = (((1,), (1,)), ((), ()))


def wait_bytes(ref, sem):
    pltpu.make_async_copy(ref, ref, sem).wait()


def kernel(
    n_z, n_rs, n_q,
    mask_hbm, pair_hbm, w_in_hbm, w_out_hbm, out_ref,
    mask_ref, pair_ref, w_in_ref, w_out_ref, load_sems, stage, send_l, send_r, l_in, r_all, l_mat, out_send, prod_in, gate,
    a2a_send, a2a_recv, ring_send, ring_recv, out_sems,
):
    loads = [
        pltpu.make_async_copy(src, dst, load_sems.at[at])
        for at, (src, dst) in enumerate(
            [(pair_hbm, pair_ref), (w_in_hbm, w_in_ref), (mask_hbm, mask_ref), (w_out_hbm, w_out_ref)]
        )
    ]
    for load in loads:
        load.start()
    n_i, n_k, width = pair_ref.shape
    half = width // 2
    n_plane = n_rs * n_q
    row_at = lax.axis_index("rows")
    q = lax.axis_index("chan")
    z = lax.div(row_at, n_rs)
    rs = lax.rem(row_at, n_rs)
    me = rs * n_q + q
    up = {"rows": lax.rem(z + 1, n_z) * n_rs + rs, "chan": q}
    down = {"rows": lax.rem(z + n_z - 1, n_z) * n_rs + rs, "chan": q}

    def plane_device(index):
        return {"rows": z * n_rs + lax.div(index, n_q), "chan": lax.rem(index, n_q)}

    barrier = pltpu.get_barrier_semaphore()

    @pl.loop(1, n_plane)
    def _(step):
        pl.semaphore_signal(
            barrier, inc=1, device_id=plane_device(lax.rem(me + step, n_plane)), device_id_type=MESH
        )

    for neighbour in (up, down):
        pl.semaphore_signal(barrier, inc=1, device_id=neighbour, device_id_type=MESH)

    loads[0].wait()
    cells = pair_ref[...].astype(jnp.float32).reshape(n_i * n_k, width)
    mean = jnp.mean(cells, axis=-1, keepdims=True)
    centered = cells - mean
    var = jnp.mean(centered * centered, axis=-1, keepdims=True)
    normed = (centered / jnp.sqrt(var + EPS)).astype(jnp.bfloat16)
    zeros = jnp.zeros((n_k, width), jnp.bfloat16)
    diag = jnp.concatenate(
        [
            jnp.concatenate(pieces, axis=1)
            for i in range(n_i)
            for block in (normed[i * n_k : (i + 1) * n_k],)
            for pieces in ((block, zeros), (zeros, block))
        ],
        axis=0,
    )
    loads[1].wait()
    w_t = w_in_ref[:, : 4 * width].astype(jnp.float32).T.astype(jnp.bfloat16)
    w_lhs = jnp.concatenate(
        [
            jnp.concatenate(
                [w_t[p * width : p * width + half], w_t[p * width + half : (p + 1) * width]], axis=1
            )
            for p in range(4)
        ],
        axis=0,
    )
    loads[2].wait()
    cell_mask = mask_ref[lax.div(row_at * n_i, BLOCK), lax.div(q * n_k, BLOCK)].astype(jnp.float32)

    def project(part, ref):
        proj = lax.dot_general(
            w_lhs[part * half : (part + 2) * half], diag, NT, preferred_element_type=jnp.float32
        )
        gated = jax.nn.sigmoid(proj[:half]) * proj[half:] * cell_mask
        for i in range(n_i):
            stage[pl.ds(i, half, stride=n_i), :] = gated[:, i * 2 * n_k : (i + 1) * 2 * n_k]
        ref[...] = stage[...].astype(jnp.bfloat16).reshape(ref.shape)

    project(2, send_r)
    pl.semaphore_wait(barrier, n_plane + 1)

    def exchange(src, dst, which):
        @pl.loop(0, n_plane - 1)
        def _(step):
            away = lax.div(step + 1, 2) * (2 * lax.rem(step, 2) - 1)
            target = lax.rem(me + n_plane // 2 + n_plane + away, n_plane)
            pltpu.make_async_remote_copy(
                src_ref=src.at[target],
                dst_ref=dst,
                send_sem=a2a_send.at[which],
                recv_sem=a2a_recv.at[which],
                device_id=plane_device(target),
                device_id_type=MESH,
            ).start()

        pltpu.make_async_copy(src.at[me], dst, a2a_recv.at[which]).start()

    exchange(send_r, r_all.at[z, q, rs], 0)
    project(0, send_l)
    exchange(send_l, l_in.at[q, rs], 1)

    gate[...] = jax.nn.sigmoid(
        jnp.dot(normed, w_in_ref[:, 4 * width :], preferred_element_type=jnp.float32)
    )

    far = n_z // 2
    n_chunks = 4
    q_chunk = n_q // n_chunks
    depth = q_chunk * 2 * n_k
    rows = n_rs * n_i

    def origin(direction, step):
        return lax.rem(z + (n_z - step if direction == 0 else step), n_z)

    def ring_copy(direction, step, chunk, block):
        ref = r_all.at[block, pl.ds(chunk * q_chunk, q_chunk)]
        return pltpu.make_async_remote_copy(
            src_ref=ref,
            dst_ref=ref,
            send_sem=ring_send.at[direction, step, chunk],
            recv_sem=ring_recv.at[direction, step, chunk],
            device_id=up if direction == 0 else down,
            device_id_type=MESH,
        )

    def carried(direction, step):
        if step + 1 < far:
            return range(n_chunks)
        return range(0, n_chunks // 2) if direction == 0 else range(n_chunks // 2, n_chunks)

    started = []

    def forward(direction, step, chunk):
        if step < far and chunk in carried(direction, step):
            copy = ring_copy(direction, step, chunk, origin(direction, step))
            copy.start()
            started.append(copy)

    def arrive(direction, step, chunk):
        ring_copy(direction, step - 1, chunk, origin(direction, step)).wait_recv()
        forward(direction, step, chunk)

    def product(block, chunk):
        right = jnp.concatenate(
            [r_all[block, chunk * q_chunk + k].reshape(rows, 2 * n_k) for k in range(q_chunk)], axis=1
        )
        return lax.dot_general(
            l_mat[:, chunk * depth : (chunk + 1) * depth], right, NT, preferred_element_type=jnp.float32
        )

    def emit(prod, block, slot):
        joined = jnp.concatenate([prod[:rows], prod[rows:]], axis=1).astype(jnp.bfloat16)
        out_send[slot] = joined.reshape(n_rs, n_i, 2 * n_k)

        @pl.loop(0, n_rs)
        def _(step):
            target = lax.rem(rs + n_rs // 2 + step, n_rs)
            local = jnp.logical_and(target == rs, block == q)

            @pl.when(local)
            def _():
                pltpu.make_async_copy(
                    out_send.at[slot, target], prod_in.at[me], out_sems.at[1]
                ).start()

            @pl.when(jnp.logical_not(local))
            def _():
                pltpu.make_async_remote_copy(
                    src_ref=out_send.at[slot, target],
                    dst_ref=prod_in.at[me],
                    send_sem=out_sems.at[0],
                    recv_sem=out_sems.at[1],
                    device_id={"rows": z * n_rs + target, "chan": block},
                    device_id_type=MESH,
                ).start()

    def multiply(direction, step):
        block = origin(direction, step)
        total = product(block, 0)
        for chunk in range(1, n_chunks):
            total = total + product(block, chunk)
        emit(total, block, 2 * step - direction)

    wait_bytes(r_all.at[z], a2a_recv.at[0])
    for chunk in range(n_chunks):
        for direction in (0, 1):
            forward(direction, 0, chunk)

    for step in range(1, far):
        for chunk in range(n_chunks):
            for direction in (0, 1):
                arrive(direction, step, chunk)
            if step > 1 and chunk in (0, n_chunks // 2):
                multiply(0 if chunk == 0 else 1, step - 1)
        if step == 1:
            wait_bytes(l_in, a2a_recv.at[1])
            low = lax.broadcasted_iota(jnp.int32, (rows, 2 * n_k), 1) < n_k
            for k in range(n_q):
                block = l_in[k].reshape(rows, 2 * n_k).astype(jnp.float32)
                both = jnp.concatenate(
                    [jnp.where(low, block, 0.0), jnp.where(low, 0.0, block)], axis=0
                )
                l_mat[:, k * 2 * n_k : (k + 1) * 2 * n_k] = both.astype(jnp.bfloat16)
            multiply(0, 0)

    last = origin(0, far)
    total = None
    pairs = zip(carried(0, far - 1), carried(1, far - 1), strict=True)
    for at, chunks in enumerate(pairs):
        for direction in (0, 1):
            arrive(direction, far, chunks[direction])
            part = product(last, chunks[direction])
            total = part if total is None else total + part
        if at == 0:
            multiply(0, far - 1)
            multiply(1, far - 1)
    emit(total, last, 2 * far - 1)

    loads[3].wait()
    w_halves = jnp.concatenate([w_out_ref[:half], w_out_ref[half:]], axis=1)
    wait_bytes(prod_in, out_sems.at[1])
    stage[...] = prod_in[...].astype(jnp.float32).reshape(n_plane * n_i, 2 * n_k)
    turned = []
    for i in range(n_i):
        values = stage[pl.ds(i, half, stride=n_i), :]
        total = jnp.sum(values, axis=0, keepdims=True)
        mean = (total + pltpu.roll(total, n_k, 1)) * (1.0 / width)
        centered = values - mean
        square = jnp.sum(centered * centered, axis=0, keepdims=True)
        var = (square + pltpu.roll(square, n_k, 1)) * (1.0 / width)
        turned.append((centered / jnp.sqrt(var + EPS)).T.astype(jnp.bfloat16))
    mixed = jnp.dot(
        jnp.concatenate(turned, axis=0), w_halves, preferred_element_type=jnp.float32
    )
    for i in range(n_i):
        at = i * 2 * n_k
        summed = mixed[at : at + n_k, :width] + mixed[at + n_k : at + 2 * n_k, width:]
        out_ref[i] = (gate[i * n_k : (i + 1) * n_k] * summed).astype(jnp.bfloat16)

    others = pl.ds(0, n_plane - 1)
    wait_bytes(send_r.at[others], a2a_send.at[0])
    wait_bytes(send_l.at[others], a2a_send.at[1])
    for copy in started:
        copy.wait_send()

    wait_bytes(prod_in.at[others], out_sems.at[0])


def solution(mesh):
    n_rows, n_q = mesh.shape["rows"], mesh.shape["chan"]

    def on_device(pair, block_mask, w_in, w_out):
        n_i, n_k, width = pair.shape
        half = width // 2
        n_rs = half // n_q
        n_z = n_rows // n_rs
        n_plane = n_rs * n_q
        tile = (n_i, 2 * n_k)
        hbm = pl.BlockSpec(memory_space=pltpu.HBM)
        return pl.pallas_call(
            functools.partial(kernel, n_z, n_rs, n_q),
            out_shape=jax.ShapeDtypeStruct((n_i, n_k, width), jnp.bfloat16),
            in_specs=[hbm] * 4,
            out_specs=pl.BlockSpec(memory_space=pltpu.VMEM),
            scratch_shapes=[
                pltpu.SMEM(block_mask.shape, block_mask.dtype),
                pltpu.VMEM(pair.shape, pair.dtype),
                pltpu.VMEM(w_in.shape, w_in.dtype),
                pltpu.VMEM(w_out.shape, w_out.dtype),
                pltpu.SemaphoreType.DMA((4,)),
                pltpu.VMEM((n_plane * n_i, 2 * n_k), jnp.float32),
                pltpu.VMEM((n_plane, *tile), jnp.bfloat16),
                pltpu.VMEM((n_plane, *tile), jnp.bfloat16),
                pltpu.VMEM((n_q, n_rs, *tile), jnp.bfloat16),
                pltpu.VMEM((n_z, n_q, n_rs, *tile), jnp.bfloat16),
                pltpu.VMEM((2 * n_rs * n_i, n_q * 2 * n_k), jnp.bfloat16),
                pltpu.VMEM((n_z, n_rs, *tile), jnp.bfloat16),
                pltpu.VMEM((n_plane, *tile), jnp.bfloat16),
                pltpu.VMEM((n_i * n_k, width), jnp.float32),
                pltpu.SemaphoreType.DMA((2,)),
                pltpu.SemaphoreType.DMA((2,)),
                pltpu.SemaphoreType.DMA((2, n_z // 2, 4)),
                pltpu.SemaphoreType.DMA((2, n_z // 2, 4)),
                pltpu.SemaphoreType.DMA((2,)),
            ],
            compiler_params=pltpu.CompilerParams(
                collective_id=0, has_side_effects=True, vmem_limit_bytes=16 * 2**20
            ),
        )(*(pltpu.with_memory_space_constraint(x, pltpu.HBM) for x in (block_mask, pair, w_in, w_out)))

    placed = (P("rows", "chan", None), P(), P(), P())
    return jax.shard_map(
        on_device, mesh=mesh, in_specs=placed, out_specs=P("rows", "chan", None), check_vma=False
    )
```

```python
import functools

import jax
import jax.numpy as jnp
from jax import lax
from jax.experimental import pallas as pl
from jax.experimental.pallas import tpu as pltpu
from jax.sharding import PartitionSpec as P

BLOCK = 128
EPS = 1e-05
CORES = 2
UNROLL = 4
MESH = pl.DeviceIdType.MESH
NT = (((1,), (1,)), ((), ()))


def wait_bytes(ref, sem):
    pltpu.make_async_copy(ref, ref, sem).wait()


def kernel(
    n_z, n_rs, n_q,
    mask_hbm, pair_hbm, w_in_hbm, w_out_hbm, out_ref,
    mask_ref, pair_ref, w_in_ref, w_out_ref, load_sems, stage, send_l, send_r, l_in, r_all, l_mat, out_send, prod_in, gate,
    a2a_send, a2a_recv, ring_send, ring_recv, out_sems,
    near_sem, far_sem,
):
    loads = [
        pltpu.make_async_copy(src, dst, load_sems.at[at])
        for at, (src, dst) in enumerate(
            [(pair_hbm, pair_ref), (w_in_hbm, w_in_ref), (mask_hbm, mask_ref), (w_out_hbm, w_out_ref)]
        )
    ]
    for load in loads:
        load.start()
    n_i, n_k, width = pair_ref.shape
    half = width // 2
    n_plane = n_rs * n_q
    row_at = lax.axis_index("rows")
    q = lax.axis_index("chan")
    z = lax.div(row_at, n_rs)
    rs = lax.rem(row_at, n_rs)
    me = rs * n_q + q
    up = {"rows": lax.rem(z + 1, n_z) * n_rs + rs, "chan": q}
    down = {"rows": lax.rem(z + n_z - 1, n_z) * n_rs + rs, "chan": q}

    def plane_device(index):
        return {"rows": z * n_rs + lax.div(index, n_q), "chan": lax.rem(index, n_q)}

    n_parts = r_all.shape[1]
    group = lax.div(rs, CORES)
    core = lax.rem(rs, CORES)
    n_group = CORES * n_q
    opposite = n_parts // 2
    near_first = sorted(range(n_parts), key=lambda part: min(part, n_parts - part))
    partner = {"rows": row_at + 1 - 2 * core, "chan": q}
    barrier = pltpu.get_barrier_semaphore()

    def hello(device):
        pl.semaphore_signal(barrier, inc=1, device_id=device, device_id_type=MESH)

    for part in near_first[::-1]:
        first = z * n_rs + lax.rem(group + part, n_parts) * CORES + (1 if part == opposite else 0)

        @pl.loop(1 if part == 0 else 0, n_q, unroll=True)
        def _(step):
            hello({"rows": first, "chan": lax.rem(q + step, n_q)})

    hello(partner)
    for neighbour in (up, down):
        hello({"rows": neighbour["rows"] - core, "chan": q})

    loads[0].wait()
    cells = pair_ref[...].astype(jnp.float32).reshape(n_i * n_k, width)
    mean = jnp.mean(cells, axis=-1, keepdims=True)
    centered = cells - mean
    var = jnp.mean(centered * centered, axis=-1, keepdims=True)
    normed = (centered / jnp.sqrt(var + EPS)).astype(jnp.bfloat16)
    zeros = jnp.zeros((n_k, width), jnp.bfloat16)
    diag = jnp.concatenate(
        [
            jnp.concatenate(pieces, axis=1)
            for i in range(n_i)
            for block in (normed[i * n_k : (i + 1) * n_k],)
            for pieces in ((block, zeros), (zeros, block))
        ],
        axis=0,
    )
    loads[1].wait()
    w_t = w_in_ref[:, : 4 * width].astype(jnp.float32).T.astype(jnp.bfloat16)
    w_lhs = jnp.concatenate(
        [
            jnp.concatenate(
                [w_t[p * width : p * width + half], w_t[p * width + half : (p + 1) * width]], axis=1
            )
            for p in range(4)
        ],
        axis=0,
    )
    loads[2].wait()
    cell_mask = mask_ref[lax.div(row_at * n_i, BLOCK), lax.div(q * n_k, BLOCK)].astype(jnp.float32)

    def project(part, ref):
        proj = lax.dot_general(
            w_lhs[part * half : (part + 2) * half], diag, NT, preferred_element_type=jnp.float32
        )
        gated = jax.nn.sigmoid(proj[:half]) * proj[half:] * cell_mask
        for i in range(n_i):
            stage[pl.ds(i, half, stride=n_i), :] = gated[:, i * 2 * n_k : (i + 1) * 2 * n_k]
        ref[...] = stage[...].astype(jnp.bfloat16).reshape(ref.shape)

    project(2, send_r)

    def tell(sem):
        pl.semaphore_signal(sem, inc=1, device_id=partner, device_id_type=MESH)

    def send(src, target, dst, send_sem, recv_sem):
        pltpu.make_async_remote_copy(
            src_ref=src.at[target],
            dst_ref=dst,
            send_sem=send_sem,
            recv_sem=recv_sem,
            device_id=plane_device(target),
            device_id_type=MESH,
        ).start()

    r_slot = r_all.at[z, group, core, q]

    def send_group(part):
        target_group = lax.rem(group + part, n_parts)

        @pl.loop(1 if part == 0 else 0, n_group, unroll=UNROLL)
        def _(step):
            to = lax.rem(core * n_q + q + step, n_group)
            pltpu.make_async_remote_copy(
                src_ref=send_r.at[target_group * n_group + to],
                dst_ref=r_slot,
                send_sem=a2a_send.at[0],
                recv_sem=a2a_recv.at[(n_parts - part) % n_parts],
                device_id={
                    "rows": z * n_rs + target_group * CORES + lax.div(to, n_q),
                    "chan": lax.rem(to, n_q),
                },
                device_id_type=MESH,
            ).start()

    @pl.when(core == 0)
    def _():
        pl.semaphore_wait(barrier, n_plane - n_group - 1 + 2 * CORES)
        tell(near_sem)

    @pl.when(core == 1)
    def _():
        pl.semaphore_wait(near_sem, 1)

    pltpu.make_async_copy(send_r.at[me], r_slot, a2a_recv.at[0]).start()
    for part in near_first[-2::-1]:
        send_group(part)

    @pl.when(core == 1)
    def _():
        pl.semaphore_wait(barrier, n_group + 1)
        tell(far_sem)

    @pl.when(core == 0)
    def _():
        pl.semaphore_wait(far_sem, 1)

    send_group(opposite)

    project(0, send_l)

    gate[...] = jax.nn.sigmoid(
        jnp.dot(normed, w_in_ref[:, 4 * width :], preferred_element_type=jnp.float32)
    )

    far = n_z // 2
    rows = n_rs * n_i

    def origin(direction, step):
        return lax.rem(z + (n_z - step if direction == 0 else step), n_z)

    def ring_copy(direction, step, chunk, block):
        ref = r_all.at[block, lax.rem(group + chunk, n_parts)]
        return pltpu.make_async_remote_copy(
            src_ref=ref,
            dst_ref=ref,
            send_sem=ring_send.at[direction, step, chunk],
            recv_sem=ring_recv.at[direction, step, chunk],
            device_id=up if direction == 0 else down,
            device_id_type=MESH,
        )

    def carried(direction, step):
        if step + 1 < far:
            return near_first
        return near_first[direction::2]

    started = []

    def forward(direction, step, chunk):
        if step < far and chunk in carried(direction, step):
            copy = ring_copy(direction, step, chunk, origin(direction, step))
            copy.start()
            started.append(copy)

    def arrive(direction, step, chunk):
        ring_copy(direction, step - 1, chunk, origin(direction, step)).wait_recv()
        forward(direction, step, chunk)

    def emit(prod, block, slot):
        joined = jnp.concatenate([prod[:rows], prod[rows:]], axis=1).astype(jnp.bfloat16)
        out_send[slot] = joined.reshape(n_rs, n_i, 2 * n_k)

        @pl.loop(0, n_rs)
        def _(step):
            target = lax.rem(rs + n_rs // 2 + step, n_rs)
            local = jnp.logical_and(target == rs, block == q)

            @pl.when(local)
            def _():
                pltpu.make_async_copy(
                    out_send.at[slot, target], prod_in.at[me], out_sems.at[1]
                ).start()

            @pl.when(jnp.logical_not(local))
            def _():
                pltpu.make_async_remote_copy(
                    src_ref=out_send.at[slot, target],
                    dst_ref=prod_in.at[me],
                    send_sem=out_sems.at[0],
                    recv_sem=out_sems.at[1],
                    device_id={"rows": z * n_rs + target, "chan": block},
                    device_id_type=MESH,
                ).start()

    def multiply(direction, step):
        block = origin(direction, step)
        right = jnp.concatenate(
            [r_all[block, :, :, k].reshape(rows, 2 * n_k) for k in range(n_q)], axis=1
        )
        total = lax.dot_general(l_mat[...], right, NT, preferred_element_type=jnp.float32)
        emit(total, block, max(2 * step - direction, 0))

    for chunk in near_first:
        wait_bytes(r_all.at[z, lax.rem(group + chunk, n_parts)], a2a_recv.at[chunk])
        for direction in (0, 1):
            forward(direction, 0, chunk)
        if chunk == near_first[0]:
            pltpu.make_async_copy(send_l.at[me], l_in.at[q, rs], a2a_recv.at[n_parts]).start()

            @pl.loop(0, n_plane - 1)
            def _(step):
                away = lax.div(step + 1, 2) * (2 * lax.rem(step, 2) - 1)
                target = lax.rem(me + n_plane // 2 + n_plane + away, n_plane)
                send(send_l, target, l_in.at[q, rs], a2a_send.at[1], a2a_recv.at[n_parts])

    for step in range(1, far):
        for at, chunk in enumerate(near_first):
            for direction in (0, 1):
                arrive(direction, step, chunk)
            if step > 1 and at % 2 == 0:
                multiply(at // 2, step - 1)
        if step == 1:
            wait_bytes(l_in, a2a_recv.at[n_parts])
            low = lax.broadcasted_iota(jnp.int32, (rows, 2 * n_k), 1) < n_k
            for k in range(n_q):
                block = l_in[k].reshape(rows, 2 * n_k).astype(jnp.float32)
                both = jnp.concatenate(
                    [jnp.where(low, block, 0.0), jnp.where(low, 0.0, block)], axis=0
                )
                l_mat[:, k * 2 * n_k : (k + 1) * 2 * n_k] = both.astype(jnp.bfloat16)
            multiply(0, 0)

    for direction in (0, 1):
        multiply(direction, far - 1)
    for pair in zip(carried(0, far - 1), carried(1, far - 1), strict=True):
        for direction in (0, 1):
            arrive(direction, far, pair[direction])
    multiply(1, far)

    loads[3].wait()
    w_halves = jnp.concatenate([w_out_ref[:half], w_out_ref[half:]], axis=1)
    wait_bytes(prod_in, out_sems.at[1])
    stage[...] = prod_in[...].astype(jnp.float32).reshape(n_plane * n_i, 2 * n_k)
    turned = []
    for i in range(n_i):
        values = stage[pl.ds(i, half, stride=n_i), :]
        total = jnp.sum(values, axis=0, keepdims=True)
        mean = (total + pltpu.roll(total, n_k, 1)) * (1.0 / width)
        centered = values - mean
        square = jnp.sum(centered * centered, axis=0, keepdims=True)
        var = (square + pltpu.roll(square, n_k, 1)) * (1.0 / width)
        turned.append((centered / jnp.sqrt(var + EPS)).T.astype(jnp.bfloat16))
    mixed = jnp.dot(
        jnp.concatenate(turned, axis=0), w_halves, preferred_element_type=jnp.float32
    )
    for i in range(n_i):
        at = i * 2 * n_k
        summed = mixed[at : at + n_k, :width] + mixed[at + n_k : at + 2 * n_k, width:]
        out_ref[i] = (gate[i * n_k : (i + 1) * n_k] * summed).astype(jnp.bfloat16)

    others = pl.ds(0, n_plane - 1)
    wait_bytes(send_r.at[others], a2a_send.at[0])
    wait_bytes(send_l.at[others], a2a_send.at[1])
    for copy in started:
        copy.wait_send()

    wait_bytes(prod_in.at[others], out_sems.at[0])


def solution(mesh):
    n_rows, n_q = mesh.shape["rows"], mesh.shape["chan"]

    def on_device(pair, block_mask, w_in, w_out):
        n_i, n_k, width = pair.shape
        half = width // 2
        n_rs = half // n_q
        n_z = n_rows // n_rs
        n_plane = n_rs * n_q
        tile = (n_i, 2 * n_k)
        hbm = pl.BlockSpec(memory_space=pltpu.HBM)
        return pl.pallas_call(
            functools.partial(kernel, n_z, n_rs, n_q),
            out_shape=jax.ShapeDtypeStruct((n_i, n_k, width), jnp.bfloat16),
            in_specs=[hbm] * 4,
            out_specs=pl.BlockSpec(memory_space=pltpu.VMEM),
            scratch_shapes=[
                pltpu.SMEM(block_mask.shape, block_mask.dtype),
                pltpu.VMEM(pair.shape, pair.dtype),
                pltpu.VMEM(w_in.shape, w_in.dtype),
                pltpu.VMEM(w_out.shape, w_out.dtype),
                pltpu.SemaphoreType.DMA((4,)),
                pltpu.VMEM((n_plane * n_i, 2 * n_k), jnp.float32),
                pltpu.VMEM((n_plane, *tile), jnp.bfloat16),
                pltpu.VMEM((n_plane, *tile), jnp.bfloat16),
                pltpu.VMEM((n_q, n_rs, *tile), jnp.bfloat16),
                pltpu.VMEM((n_z, n_rs // CORES, CORES, n_q, *tile), jnp.bfloat16),
                pltpu.VMEM((2 * n_rs * n_i, n_q * 2 * n_k), jnp.bfloat16),
                pltpu.VMEM((n_z, n_rs, *tile), jnp.bfloat16),
                pltpu.VMEM((n_plane, *tile), jnp.bfloat16),
                pltpu.VMEM((n_i * n_k, width), jnp.float32),
                pltpu.SemaphoreType.DMA((2,)),
                pltpu.SemaphoreType.DMA((n_rs // CORES + 1,)),
                pltpu.SemaphoreType.DMA((2, n_z // 2, n_rs // CORES)),
                pltpu.SemaphoreType.DMA((2, n_z // 2, n_rs // CORES)),
                pltpu.SemaphoreType.DMA((2,)),
                pltpu.SemaphoreType.REGULAR,
                pltpu.SemaphoreType.REGULAR,
            ],
            compiler_params=pltpu.CompilerParams(
                collective_id=0, has_side_effects=True, vmem_limit_bytes=16 * 2**20
            ),
        )(*(pltpu.with_memory_space_constraint(x, pltpu.HBM) for x in (block_mask, pair, w_in, w_out)))

    placed = (P("rows", "chan", None), P(), P(), P())
    return jax.shard_map(
        on_device, mesh=mesh, in_specs=placed, out_specs=P("rows", "chan", None), check_vma=False
    )
```

```python
import functools

import jax
import jax.numpy as jnp
from jax import lax
from jax.experimental import pallas as pl
from jax.experimental.pallas import tpu as pltpu
from jax.sharding import PartitionSpec as P

BLOCK = 128
EPS = 1e-05
CORES = 2
UNROLL = 4
UNROLL_L = 7
SEND_LEFT = 1
LEFT_STEP = 1
POPS = 2
MESH = pl.DeviceIdType.MESH
NT = (((1,), (1,)), ((), ()))


def wait_bytes(ref, sem):
    pltpu.make_async_copy(ref, ref, sem).wait()


def kernel(
    n_z, n_rs, n_q,
    mask_hbm, pair_hbm, w_in_hbm, w_out_hbm, out_ref,
    mask_ref, pair_ref, w_in_ref, w_out_ref, load_sems, stage, send_l, send_r, l_in, r_all, l_mat, out_send, prod_in, gate,
    a2a_send, a2a_recv, ring_send, ring_recv, out_sems,
    near_sem, far_sem,
):
    loads = [
        pltpu.make_async_copy(src, dst, load_sems.at[at])
        for at, (src, dst) in enumerate(
            [(pair_hbm, pair_ref), (w_in_hbm, w_in_ref), (mask_hbm, mask_ref), (w_out_hbm, w_out_ref)]
        )
    ]
    for load in loads:
        load.start()
    n_i, n_k, width = pair_ref.shape
    half = width // 2
    n_plane = n_rs * n_q
    row_at = lax.axis_index("rows")
    q = lax.axis_index("chan")
    z = lax.div(row_at, n_rs)
    rs = lax.rem(row_at, n_rs)
    me = rs * n_q + q
    up = {"rows": lax.rem(z + 1, n_z) * n_rs + rs, "chan": q}
    down = {"rows": lax.rem(z + n_z - 1, n_z) * n_rs + rs, "chan": q}

    def plane_device(index):
        return {"rows": z * n_rs + lax.div(index, n_q), "chan": lax.rem(index, n_q)}

    n_parts = r_all.shape[1]
    group = lax.div(rs, CORES)
    core = lax.rem(rs, CORES)
    n_group = CORES * n_q
    opposite = n_parts // 2
    near_first = sorted(range(n_parts), key=lambda part: min(part, n_parts - part))
    partner = {"rows": row_at + 1 - 2 * core, "chan": q}
    barrier = pltpu.get_barrier_semaphore()

    def hello(device):
        pl.semaphore_signal(barrier, inc=1, device_id=device, device_id_type=MESH)

    for part in near_first[::-1]:
        first = z * n_rs + lax.rem(group + part, n_parts) * CORES + (1 if part == opposite else 0)

        @pl.loop(1 if part == 0 else 0, n_q, unroll=True)
        def _(step):
            hello({"rows": first, "chan": lax.rem(q + step, n_q)})

    hello(partner)
    for neighbour in (up, down):
        hello({"rows": neighbour["rows"] - core, "chan": q})

    loads[0].wait()
    cells = pair_ref[...].astype(jnp.float32).reshape(n_i * n_k, width)
    mean = jnp.mean(cells, axis=-1, keepdims=True)
    centered = cells - mean
    var = jnp.mean(centered * centered, axis=-1, keepdims=True)
    normed = (centered / jnp.sqrt(var + EPS)).astype(jnp.bfloat16)
    zeros = jnp.zeros((n_k, width), jnp.bfloat16)
    diag = jnp.concatenate(
        [
            jnp.concatenate(pieces, axis=1)
            for i in range(n_i)
            for block in (normed[i * n_k : (i + 1) * n_k],)
            for pieces in ((block, zeros), (zeros, block))
        ],
        axis=0,
    )
    loads[1].wait()
    w_t = w_in_ref[:, : 4 * width].astype(jnp.float32).T.astype(jnp.bfloat16)
    w_lhs = jnp.concatenate(
        [
            jnp.concatenate(
                [w_t[p * width : p * width + half], w_t[p * width + half : (p + 1) * width]], axis=1
            )
            for p in range(4)
        ],
        axis=0,
    )
    loads[2].wait()
    cell_mask = mask_ref[lax.div(row_at * n_i, BLOCK), lax.div(q * n_k, BLOCK)].astype(jnp.float32)

    def project(part, ref):
        proj = lax.dot_general(
            w_lhs[part * half : (part + 2) * half], diag, NT, preferred_element_type=jnp.float32
        )
        gated = jax.nn.sigmoid(proj[:half]) * proj[half:] * cell_mask
        for i in range(n_i):
            stage[pl.ds(i, half, stride=n_i), :] = gated[:, i * 2 * n_k : (i + 1) * 2 * n_k]
        ref[...] = stage[...].astype(jnp.bfloat16).reshape(ref.shape)

    project(2, send_r)

    def tell(sem):
        pl.semaphore_signal(sem, inc=1, device_id=partner, device_id_type=MESH)

    def send(src, target, dst, send_sem, recv_sem):
        pltpu.make_async_remote_copy(
            src_ref=src.at[target],
            dst_ref=dst,
            send_sem=send_sem,
            recv_sem=recv_sem,
            device_id=plane_device(target),
            device_id_type=MESH,
        ).start()

    r_slot = r_all.at[z, group, core, q]

    def send_group(part):
        target_group = lax.rem(group + part, n_parts)

        @pl.loop(1 if part == 0 else 0, n_group, unroll=UNROLL)
        def _(step):
            to = lax.rem(core * n_q + q + step, n_group)
            pltpu.make_async_remote_copy(
                src_ref=send_r.at[target_group * n_group + to],
                dst_ref=r_slot,
                send_sem=a2a_send.at[0],
                recv_sem=a2a_recv.at[(n_parts - part) % n_parts],
                device_id={
                    "rows": z * n_rs + target_group * CORES + lax.div(to, n_q),
                    "chan": lax.rem(to, n_q),
                },
                device_id_type=MESH,
            ).start()

    @pl.when(core == 0)
    def _():
        pl.semaphore_wait(barrier, n_plane - n_group - 1 + 2 * CORES)
        tell(near_sem)

    @pl.when(core == 1)
    def _():
        pl.semaphore_wait(near_sem, 1)

    pltpu.make_async_copy(send_r.at[me], r_slot, a2a_recv.at[0]).start()
    def hear_far():
        @pl.when(core == 1)
        def _():
            pl.semaphore_wait(barrier, n_group + 1)
            tell(far_sem)

        @pl.when(core == 0)
        def _():
            pl.semaphore_wait(far_sem, 1)

    @pl.when(group == opposite)
    def _():
        hear_far()
        send_group(opposite)

    for part in near_first[-2::-1]:
        send_group(part)

    @pl.when(group != opposite)
    def _():
        hear_far()
        send_group(opposite)


    project(0, send_l)

    gate[...] = jax.nn.sigmoid(
        jnp.dot(normed, w_in_ref[:, 4 * width :], preferred_element_type=jnp.float32)
    )

    far = n_z // 2
    rows = n_rs * n_i

    def origin(direction, step):
        return lax.rem(z + (n_z - step if direction == 0 else step), n_z)

    def ring_copy(direction, step, chunk, block):
        ref = r_all.at[block, lax.rem(group + chunk, n_parts)]
        return pltpu.make_async_remote_copy(
            src_ref=ref,
            dst_ref=ref,
            send_sem=ring_send.at[direction, step, chunk],
            recv_sem=ring_recv.at[direction, step, chunk],
            device_id=up if direction == 0 else down,
            device_id_type=MESH,
        )

    def carried(direction, step):
        if step + 1 < far:
            return near_first
        return near_first[direction::2]

    started = []

    def forward(direction, step, chunk):
        if step < far and chunk in carried(direction, step):
            copy = ring_copy(direction, step, chunk, origin(direction, step))
            copy.start()
            started.append(copy)

    def arrive(direction, step, chunk):
        ring_copy(direction, step - 1, chunk, origin(direction, step)).wait_recv()
        forward(direction, step, chunk)

    def emit(prod, block, slot):
        joined = jnp.concatenate([prod[:rows], prod[rows:]], axis=1).astype(jnp.bfloat16)
        out_send[slot] = joined.reshape(n_rs, n_i, 2 * n_k)

        @pl.loop(0, n_rs, unroll=True)
        def _(step):
            target = lax.rem(rs + n_rs // 2 + step, n_rs)
            local = jnp.logical_and(target == rs, block == q)

            @pl.when(local)
            def _():
                pltpu.make_async_copy(
                    out_send.at[slot, target], prod_in.at[me], out_sems.at[1]
                ).start()

            @pl.when(jnp.logical_not(local))
            def _():
                pltpu.make_async_remote_copy(
                    src_ref=out_send.at[slot, target],
                    dst_ref=prod_in.at[me],
                    send_sem=out_sems.at[0],
                    recv_sem=out_sems.at[1],
                    device_id={"rows": z * n_rs + target, "chan": block},
                    device_id_type=MESH,
                ).start()

    def multiply(direction, step):
        block = origin(direction, step)
        right = jnp.concatenate(
            [r_all[block, :, :, k].reshape(rows, 2 * n_k) for k in range(n_q)], axis=1
        )
        total = lax.dot_general(l_mat[...], right, NT, preferred_element_type=jnp.float32)
        emit(total, block, max(2 * step - direction, 0))

    def send_left():
        pltpu.make_async_copy(send_l.at[me], l_in.at[q, rs], a2a_recv.at[n_parts]).start()

        @pl.loop(0, n_plane - 1, unroll=UNROLL_L)
        def _(step):
            away = lax.div(step + 1, 2) * (2 * lax.rem(step, 2) - 1)
            target = lax.rem(me + n_plane // 2 + n_plane + away, n_plane)
            send(send_l, target, l_in.at[q, rs], a2a_send.at[1], a2a_recv.at[n_parts])

    def spread_left():
        wait_bytes(l_in, a2a_recv.at[n_parts])
        low = lax.broadcasted_iota(jnp.int32, (rows, 2 * n_k), 1) < n_k
        for k in range(n_q):
            block = l_in[k].reshape(rows, 2 * n_k).astype(jnp.float32)
            both = jnp.concatenate([jnp.where(low, block, 0.0), jnp.where(low, 0.0, block)], axis=0)
            l_mat[:, k * 2 * n_k : (k + 1) * 2 * n_k] = both.astype(jnp.bfloat16)
        multiply(0, 0)

    for at, part in enumerate(near_first):
        wait_bytes(r_all.at[z, lax.rem(group + part, n_parts)], a2a_recv.at[part])
        if at + 1 == SEND_LEFT:
            pl.when(core == 1)(send_left)
        for direction in (0, 1):
            forward(direction, 0, part)
        if at + 1 == SEND_LEFT:
            pl.when(core == 0)(send_left)

    work = [spread_left]
    for step in range(1, far):
        for at, part in enumerate(near_first):
            for direction in (0, 1):
                arrive(direction, step, part)
            if step > LEFT_STEP and work and at % (n_parts // POPS) == 0:
                work.pop(0)()
        work += [functools.partial(multiply, direction, step) for direction in (0, 1)]
        if step == LEFT_STEP:
            work.pop(0)()
    for item in work:
        item()
    for pair in zip(carried(0, far - 1), carried(1, far - 1), strict=True):
        for direction in (0, 1):
            arrive(direction, far, pair[direction])
    multiply(1, far)

    loads[3].wait()
    w_halves = jnp.concatenate([w_out_ref[:half], w_out_ref[half:]], axis=1)
    wait_bytes(prod_in, out_sems.at[1])
    stage[...] = prod_in[...].astype(jnp.float32).reshape(n_plane * n_i, 2 * n_k)
    turned = []
    for i in range(n_i):
        values = stage[pl.ds(i, half, stride=n_i), :]
        total = jnp.sum(values, axis=0, keepdims=True)
        mean = (total + pltpu.roll(total, n_k, 1)) * (1.0 / width)
        centered = values - mean
        square = jnp.sum(centered * centered, axis=0, keepdims=True)
        var = (square + pltpu.roll(square, n_k, 1)) * (1.0 / width)
        turned.append((centered * (1.0 / jnp.sqrt(var + EPS))).T.astype(jnp.bfloat16))
    mixed = jnp.dot(
        jnp.concatenate(turned, axis=0), w_halves, preferred_element_type=jnp.float32
    )
    for i in range(n_i):
        at = i * 2 * n_k
        summed = mixed[at : at + n_k, :width] + mixed[at + n_k : at + 2 * n_k, width:]
        out_ref[i] = (gate[i * n_k : (i + 1) * n_k] * summed).astype(jnp.bfloat16)

    others = pl.ds(0, n_plane - 1)
    wait_bytes(send_r.at[others], a2a_send.at[0])
    wait_bytes(send_l.at[others], a2a_send.at[1])
    for copy in started:
        copy.wait_send()

    wait_bytes(prod_in.at[others], out_sems.at[0])


def solution(mesh):
    n_rows, n_q = mesh.shape["rows"], mesh.shape["chan"]

    def on_device(pair, block_mask, w_in, w_out):
        n_i, n_k, width = pair.shape
        half = width // 2
        n_rs = half // n_q
        n_z = n_rows // n_rs
        n_plane = n_rs * n_q
        tile = (n_i, 2 * n_k)
        hbm = pl.BlockSpec(memory_space=pltpu.HBM)
        return pl.pallas_call(
            functools.partial(kernel, n_z, n_rs, n_q),
            out_shape=jax.ShapeDtypeStruct((n_i, n_k, width), jnp.bfloat16),
            in_specs=[hbm] * 4,
            out_specs=pl.BlockSpec(memory_space=pltpu.VMEM),
            scratch_shapes=[
                pltpu.SMEM(block_mask.shape, block_mask.dtype),
                pltpu.VMEM(pair.shape, pair.dtype),
                pltpu.VMEM(w_in.shape, w_in.dtype),
                pltpu.VMEM(w_out.shape, w_out.dtype),
                pltpu.SemaphoreType.DMA((4,)),
                pltpu.VMEM((n_plane * n_i, 2 * n_k), jnp.float32),
                pltpu.VMEM((n_plane, *tile), jnp.bfloat16),
                pltpu.VMEM((n_plane, *tile), jnp.bfloat16),
                pltpu.VMEM((n_q, n_rs, *tile), jnp.bfloat16),
                pltpu.VMEM((n_z, n_rs // CORES, CORES, n_q, *tile), jnp.bfloat16),
                pltpu.VMEM((2 * n_rs * n_i, n_q * 2 * n_k), jnp.bfloat16),
                pltpu.VMEM((n_z, n_rs, *tile), jnp.bfloat16),
                pltpu.VMEM((n_plane, *tile), jnp.bfloat16),
                pltpu.VMEM((n_i * n_k, width), jnp.float32),
                pltpu.SemaphoreType.DMA((2,)),
                pltpu.SemaphoreType.DMA((n_rs // CORES + 1,)),
                pltpu.SemaphoreType.DMA((2, n_z // 2, n_rs // CORES)),
                pltpu.SemaphoreType.DMA((2, n_z // 2, n_rs // CORES)),
                pltpu.SemaphoreType.DMA((2,)),
                pltpu.SemaphoreType.REGULAR,
                pltpu.SemaphoreType.REGULAR,
            ],
            compiler_params=pltpu.CompilerParams(
                collective_id=0, has_side_effects=True, vmem_limit_bytes=16 * 2**20
            ),
        )(*(pltpu.with_memory_space_constraint(x, pltpu.HBM) for x in (block_mask, pair, w_in, w_out)))

    placed = (P("rows", "chan", None), P(), P(), P())
    return jax.shard_map(
        on_device, mesh=mesh, in_specs=placed, out_specs=P("rows", "chan", None), check_vma=False
    )
```

```python
import functools

import jax
import jax.numpy as jnp
from jax import lax
from jax.experimental import pallas as pl
from jax.experimental.pallas import tpu as pltpu
from jax.sharding import PartitionSpec as P

BLOCK = 128
EPS = 1e-05
CORES = 2
PIECES = 4
UNROLL = 4
MESH = pl.DeviceIdType.MESH
NT = (((1,), (1,)), ((), ()))


def wait_bytes(ref, sem):
    pltpu.make_async_copy(ref, ref, sem).wait()


def kernel(
    n_z, n_rs, n_q,
    mask_hbm, pair_hbm, w_in_hbm, w_out_hbm, out_ref,
    mask_ref, pair_ref, w_in_ref, w_out_ref, load_sems, stage, send_l, send_r, l_in, r_all, l_mat, out_send, prod_in, gate,
    a2a_send, a2a_recv, ring_send, ring_recv, out_sems,
    near_sem, far_sem,
):
    loads = [
        pltpu.make_async_copy(src, dst, load_sems.at[at])
        for at, (src, dst) in enumerate(
            [(pair_hbm, pair_ref), (w_in_hbm, w_in_ref), (mask_hbm, mask_ref), (w_out_hbm, w_out_ref)]
        )
    ]
    quarter = pair_hbm.shape[0] // PIECES
    pieces = [
        pltpu.make_async_copy(
            pair_hbm.at[pl.ds(at * quarter, quarter)],
            pair_ref.at[pl.ds(at * quarter, quarter)],
            load_sems.at[4 + at],
        )
        for at in range(PIECES)
    ]
    for load in pieces + loads[1:]:
        load.start()
    n_i, n_k, width = pair_ref.shape
    half = width // 2
    n_plane = n_rs * n_q
    row_at = lax.axis_index("rows")
    q = lax.axis_index("chan")
    z = lax.div(row_at, n_rs)
    rs = lax.rem(row_at, n_rs)
    me = rs * n_q + q
    up = {"rows": lax.rem(z + 1, n_z) * n_rs + rs, "chan": q}
    down = {"rows": lax.rem(z + n_z - 1, n_z) * n_rs + rs, "chan": q}

    def plane_device(index):
        return {"rows": z * n_rs + lax.div(index, n_q), "chan": lax.rem(index, n_q)}

    n_parts = r_all.shape[1]
    group = lax.div(rs, CORES)
    core = lax.rem(rs, CORES)
    n_group = CORES * n_q
    opposite = n_parts // 2
    near_first = sorted(range(n_parts), key=lambda part: min(part, n_parts - part))
    partner = {"rows": row_at + 1 - 2 * core, "chan": q}
    barrier = pltpu.get_barrier_semaphore()

    def hello(device):
        pl.semaphore_signal(barrier, inc=1, device_id=device, device_id_type=MESH)

    for part in near_first[::-1]:
        first = z * n_rs + lax.rem(group + part, n_parts) * CORES + (1 if part == opposite else 0)

        @pl.loop(1 if part == 0 else 0, n_q, unroll=True)
        def _(step):
            hello({"rows": first, "chan": lax.rem(q + step, n_q)})

    hello(partner)
    for neighbour in (up, down):
        hello({"rows": neighbour["rows"] - core, "chan": q})

    for piece in pieces:
        piece.wait()
    cells = pair_ref[...].astype(jnp.float32).reshape(n_i * n_k, width)
    mean = jnp.mean(cells, axis=-1, keepdims=True)
    centered = cells - mean
    var = jnp.mean(centered * centered, axis=-1, keepdims=True)
    normed = (centered / jnp.sqrt(var + EPS)).astype(jnp.bfloat16)
    zeros = jnp.zeros((n_k, width), jnp.bfloat16)
    diag = jnp.concatenate(
        [
            jnp.concatenate(pieces, axis=1)
            for i in range(n_i)
            for block in (normed[i * n_k : (i + 1) * n_k],)
            for pieces in ((block, zeros), (zeros, block))
        ],
        axis=0,
    )
    loads[1].wait()
    w_t = w_in_ref[:, : 4 * width].astype(jnp.float32).T.astype(jnp.bfloat16)
    w_lhs = jnp.concatenate(
        [
            jnp.concatenate(
                [w_t[p * width : p * width + half], w_t[p * width + half : (p + 1) * width]], axis=1
            )
            for p in range(4)
        ],
        axis=0,
    )
    loads[2].wait()
    cell_mask = mask_ref[lax.div(row_at * n_i, BLOCK), lax.div(q * n_k, BLOCK)].astype(jnp.float32)

    def project(part, ref):
        proj = lax.dot_general(
            w_lhs[part * half : (part + 2) * half], diag, NT, preferred_element_type=jnp.float32
        )
        gated = jax.nn.sigmoid(proj[:half]) * proj[half:] * cell_mask
        for i in range(n_i):
            stage[pl.ds(i, half, stride=n_i), :] = gated[:, i * 2 * n_k : (i + 1) * 2 * n_k]
        ref[...] = stage[...].astype(jnp.bfloat16).reshape(ref.shape)

    project(2, send_r)

    def tell(sem):
        pl.semaphore_signal(sem, inc=1, device_id=partner, device_id_type=MESH)

    def send(src, target, dst, send_sem, recv_sem):
        pltpu.make_async_remote_copy(
            src_ref=src.at[target],
            dst_ref=dst,
            send_sem=send_sem,
            recv_sem=recv_sem,
            device_id=plane_device(target),
            device_id_type=MESH,
        ).start()

    r_slot = r_all.at[z, group, core, q]

    def send_group(part):
        target_group = lax.rem(group + part, n_parts)

        @pl.loop(1 if part == 0 else 0, n_group, unroll=UNROLL)
        def _(step):
            to = lax.rem(core * n_q + q + step, n_group)
            pltpu.make_async_remote_copy(
                src_ref=send_r.at[target_group * n_group + to],
                dst_ref=r_slot,
                send_sem=a2a_send.at[0],
                recv_sem=a2a_recv.at[(n_parts - part) % n_parts],
                device_id={
                    "rows": z * n_rs + target_group * CORES + lax.div(to, n_q),
                    "chan": lax.rem(to, n_q),
                },
                device_id_type=MESH,
            ).start()

    @pl.when(core == 0)
    def _():
        pl.semaphore_wait(barrier, n_plane - n_group - 1 + 2 * CORES)
        tell(near_sem)

    @pl.when(core == 1)
    def _():
        pl.semaphore_wait(near_sem, 1)

    pltpu.make_async_copy(send_r.at[me], r_slot, a2a_recv.at[0]).start()
    for part in near_first[-2::-1]:
        send_group(part)

    @pl.when(core == 1)
    def _():
        pl.semaphore_wait(barrier, n_group + 1)
        tell(far_sem)

    @pl.when(core == 0)
    def _():
        pl.semaphore_wait(far_sem, 1)

    send_group(opposite)

    project(0, send_l)

    gate[...] = jax.nn.sigmoid(
        jnp.dot(normed, w_in_ref[:, 4 * width :], preferred_element_type=jnp.float32)
    )

    far = n_z // 2
    rows = n_rs * n_i

    def origin(direction, step):
        return lax.rem(z + (n_z - step if direction == 0 else step), n_z)

    def ring_copy(direction, step, chunk, block):
        ref = r_all.at[block, lax.rem(group + chunk, n_parts)]
        return pltpu.make_async_remote_copy(
            src_ref=ref,
            dst_ref=ref,
            send_sem=ring_send.at[direction, step, chunk],
            recv_sem=ring_recv.at[direction, step, chunk],
            device_id=up if direction == 0 else down,
            device_id_type=MESH,
        )

    def carried(direction, step):
        if step + 1 < far:
            return near_first
        return near_first[direction::2]

    started = []

    def forward(direction, step, chunk):
        if step < far and chunk in carried(direction, step):
            copy = ring_copy(direction, step, chunk, origin(direction, step))
            copy.start()
            started.append(copy)

    def arrive(direction, step, chunk):
        ring_copy(direction, step - 1, chunk, origin(direction, step)).wait_recv()
        forward(direction, step, chunk)

    def emit(prod, block, slot):
        joined = jnp.concatenate([prod[:rows], prod[rows:]], axis=1).astype(jnp.bfloat16)
        out_send[slot] = joined.reshape(n_rs, n_i, 2 * n_k)

        @pl.loop(0, n_rs, unroll=True)
        def _(step):
            target = lax.rem(rs + n_rs // 2 + step, n_rs)
            local = jnp.logical_and(target == rs, block == q)

            @pl.when(local)
            def _():
                pltpu.make_async_copy(
                    out_send.at[slot, target], prod_in.at[me], out_sems.at[1]
                ).start()

            @pl.when(jnp.logical_not(local))
            def _():
                pltpu.make_async_remote_copy(
                    src_ref=out_send.at[slot, target],
                    dst_ref=prod_in.at[me],
                    send_sem=out_sems.at[0],
                    recv_sem=out_sems.at[1],
                    device_id={"rows": z * n_rs + target, "chan": block},
                    device_id_type=MESH,
                ).start()

    def multiply(direction, step):
        block = origin(direction, step)
        right = jnp.concatenate(
            [r_all[block, :, :, k].reshape(rows, 2 * n_k) for k in range(n_q)], axis=1
        )
        total = lax.dot_general(l_mat[...], right, NT, preferred_element_type=jnp.float32)
        emit(total, block, max(2 * step - direction, 0))

    for chunk in near_first:
        wait_bytes(r_all.at[z, lax.rem(group + chunk, n_parts)], a2a_recv.at[chunk])
        for direction in (0, 1):
            forward(direction, 0, chunk)
        if chunk == near_first[0]:
            pltpu.make_async_copy(send_l.at[me], l_in.at[q, rs], a2a_recv.at[n_parts]).start()

            @pl.loop(0, n_plane - 1)
            def _(step):
                away = lax.div(step + 1, 2) * (2 * lax.rem(step, 2) - 1)
                target = lax.rem(me + n_plane // 2 + n_plane + away, n_plane)
                send(send_l, target, l_in.at[q, rs], a2a_send.at[1], a2a_recv.at[n_parts])

    for step in range(1, far):
        for at, chunk in enumerate(near_first):
            for direction in (0, 1):
                arrive(direction, step, chunk)
            if step > 1 and at % 2 == 0:
                multiply(at // 2, step - 1)
        if step == 1:
            wait_bytes(l_in, a2a_recv.at[n_parts])
            low = lax.broadcasted_iota(jnp.int32, (rows, 2 * n_k), 1) < n_k
            for k in range(n_q):
                block = l_in[k].reshape(rows, 2 * n_k).astype(jnp.float32)
                both = jnp.concatenate(
                    [jnp.where(low, block, 0.0), jnp.where(low, 0.0, block)], axis=0
                )
                l_mat[:, k * 2 * n_k : (k + 1) * 2 * n_k] = both.astype(jnp.bfloat16)
            multiply(0, 0)

    for direction in (0, 1):
        multiply(direction, far - 1)
    for pair in zip(carried(0, far - 1), carried(1, far - 1), strict=True):
        for direction in (0, 1):
            arrive(direction, far, pair[direction])
    multiply(1, far)

    loads[3].wait()
    w_halves = jnp.concatenate([w_out_ref[:half], w_out_ref[half:]], axis=1)
    wait_bytes(prod_in, out_sems.at[1])
    stage[...] = prod_in[...].astype(jnp.float32).reshape(n_plane * n_i, 2 * n_k)
    turned = []
    for i in range(n_i):
        values = stage[pl.ds(i, half, stride=n_i), :]
        total = jnp.sum(values, axis=0, keepdims=True)
        mean = (total + pltpu.roll(total, n_k, 1)) * (1.0 / width)
        centered = values - mean
        square = jnp.sum(centered * centered, axis=0, keepdims=True)
        var = (square + pltpu.roll(square, n_k, 1)) * (1.0 / width)
        turned.append((centered / jnp.sqrt(var + EPS)).T.astype(jnp.bfloat16))
    mixed = jnp.dot(
        jnp.concatenate(turned, axis=0), w_halves, preferred_element_type=jnp.float32
    )
    for i in range(n_i):
        at = i * 2 * n_k
        summed = mixed[at : at + n_k, :width] + mixed[at + n_k : at + 2 * n_k, width:]
        out_ref[i] = (gate[i * n_k : (i + 1) * n_k] * summed).astype(jnp.bfloat16)

    others = pl.ds(0, n_plane - 1)
    wait_bytes(send_r.at[others], a2a_send.at[0])
    wait_bytes(send_l.at[others], a2a_send.at[1])
    for copy in started:
        copy.wait_send()

    wait_bytes(prod_in.at[others], out_sems.at[0])


def solution(mesh):
    n_rows, n_q = mesh.shape["rows"], mesh.shape["chan"]

    def on_device(pair, block_mask, w_in, w_out):
        n_i, n_k, width = pair.shape
        half = width // 2
        n_rs = half // n_q
        n_z = n_rows // n_rs
        n_plane = n_rs * n_q
        tile = (n_i, 2 * n_k)
        hbm = pl.BlockSpec(memory_space=pltpu.HBM)
        return pl.pallas_call(
            functools.partial(kernel, n_z, n_rs, n_q),
            out_shape=jax.ShapeDtypeStruct((n_i, n_k, width), jnp.bfloat16),
            in_specs=[hbm] * 4,
            out_specs=pl.BlockSpec(memory_space=pltpu.VMEM),
            scratch_shapes=[
                pltpu.SMEM(block_mask.shape, block_mask.dtype),
                pltpu.VMEM(pair.shape, pair.dtype),
                pltpu.VMEM(w_in.shape, w_in.dtype),
                pltpu.VMEM(w_out.shape, w_out.dtype),
                pltpu.SemaphoreType.DMA((4 + PIECES,)),
                pltpu.VMEM((n_plane * n_i, 2 * n_k), jnp.float32),
                pltpu.VMEM((n_plane, *tile), jnp.bfloat16),
                pltpu.VMEM((n_plane, *tile), jnp.bfloat16),
                pltpu.VMEM((n_q, n_rs, *tile), jnp.bfloat16),
                pltpu.VMEM((n_z, n_rs // CORES, CORES, n_q, *tile), jnp.bfloat16),
                pltpu.VMEM((2 * n_rs * n_i, n_q * 2 * n_k), jnp.bfloat16),
                pltpu.VMEM((n_z, n_rs, *tile), jnp.bfloat16),
                pltpu.VMEM((n_plane, *tile), jnp.bfloat16),
                pltpu.VMEM((n_i * n_k, width), jnp.float32),
                pltpu.SemaphoreType.DMA((2,)),
                pltpu.SemaphoreType.DMA((n_rs // CORES + 1,)),
                pltpu.SemaphoreType.DMA((2, n_z // 2, n_rs // CORES)),
                pltpu.SemaphoreType.DMA((2, n_z // 2, n_rs // CORES)),
                pltpu.SemaphoreType.DMA((2,)),
                pltpu.SemaphoreType.REGULAR,
                pltpu.SemaphoreType.REGULAR,
            ],
            compiler_params=pltpu.CompilerParams(
                collective_id=0, has_side_effects=True, vmem_limit_bytes=16 * 2**20
            ),
        )(*(pltpu.with_memory_space_constraint(x, pltpu.HBM) for x in (block_mask, pair, w_in, w_out)))

    placed = (P("rows", "chan", None), P(), P(), P())
    return jax.shard_map(
        on_device, mesh=mesh, in_specs=placed, out_specs=P("rows", "chan", None), check_vma=False
    )
```
